32 devices in a mesh: depth: 4 (over z), dp: 8 (over y, x, core).
Axes of the slice: x: 2, y: 2, z: 4, core: 2. Of those that a mesh axis runs over, the one named last changes fastest.
Arguments:
- layer_inputs: float32 [4, 3072, 2048], P('depth', 'dp'), may hold values from -6 to 6
- weights: float32 [4, 2048, 2048], P('depth', 'dp'), may hold values from -6 to 6
- offsets: float32 [4, 2048], P('depth', 'dp'), may hold values from -3 to 3
- layer_outputs: float32 [4, 3072, 2048], P('depth', 'dp'), may hold values from 0 to 2
- multipliers: float32 [4, 3072, 2048], P('depth', 'dp'), may hold values from -3 to 3
Outputs:
- new_inputs: float32 [4, 3072, 2048], P('depth', 'dp')
- new_weights: float32 [4, 2048, 2048], P('depth', 'dp')
- new_offsets: float32 [4, 2048], P('depth', 'dp')
- new_outputs: float32 [4, 3072, 2048], P('depth', 'dp')
- new_multipliers: float32 [4, 3072, 2048], P('depth', 'dp')
The draws below stay inside these ranges and needn't reach their ends.
All inputs are finite; a program needn't handle non-finite values.
Results may differ from the reference program's by a relative error of at most 0.00008.
Values sent between devices are 32-bit elements; how exact they have to be, the bound alone decides.
A program may use at most 128 MiB of HBM per device.

```python
import math
import jax
import jax.numpy as jnp
from jax import lax

D = 2048
LAYERS = 4
SAMPLES = 3072


def block_scale(key, extent, pieces, smallest, high):
    level = 1.0
    for position, parts in pieces:
        draws = jax.random.uniform(jax.random.fold_in(jax.random.fold_in(key, 6), position), (parts,), jnp.float32, smallest / len(pieces), high / len(pieces))
        level = level * jnp.repeat(jnp.exp(draws), extent[position] // parts).reshape((-1,) + (1,) * (len(extent) - 1 - position))
    return level


def centred(key, shape, spread, most, shards=(), held_as=jnp.bfloat16):
    result = jax.random.normal(key, shape, jnp.float32) * spread
    if len(shards) > 0:
        result = block_scale(key, shape, shards, -0.22, 0.18) * result
    return jnp.clip(result, min=-most, max=most).astype(held_as)


def setup_inputs(seed: int = 0) -> dict:
    streams_of = jax.random.split(jax.random.key(seed), 6)
    return {
        "layer_inputs": centred(streams_of[0], (LAYERS, SAMPLES, D), 1.0, 6.0, ((0, 4), (1, 8)), jnp.float32),
        "weights": centred(streams_of[1], (LAYERS, D, D), 1.0, 6.0, ((0, 4), (1, 8)), jnp.float32),
        "offsets": centred(streams_of[2], (LAYERS, D), 0.5, 3.0, ((0, 4), (1, 8)), jnp.float32),
        "layer_outputs": jnp.clip(2.0 * jax.random.uniform(streams_of[3], (LAYERS, SAMPLES, D), jnp.float32) ** block_scale(streams_of[3], (LAYERS, SAMPLES, D), ((0, 4), (1, 8)), -0.2, 0.2), 0.0, 2.0),
        "multipliers": centred(streams_of[4], (LAYERS, SAMPLES, D), 0.5, 3.0, ((0, 4), (1, 8)), jnp.float32),
    }


fit_weight = 1.0
penalty = 1.0
step_input = 0.5

def reference(layer_inputs, weights, offsets, layer_outputs, multipliers):
    highest = lax.Precision.HIGHEST
    scaling = 1.0 / math.sqrt(D)
    samples = layer_inputs.shape[1]
    step_weight = 8.0 / math.sqrt(samples)
    step_offset = 0.5 / math.sqrt(samples)
    affine = scaling * jnp.einsum('lsd,lkd->lsk', layer_inputs, weights, precision=highest) + offsets[:, None, :]
    misfit = affine - layer_outputs
    pulled = scaling * jnp.einsum('lsk,lkd->lsd', misfit, weights, precision=highest)
    zero_layer = jnp.zeros_like(layer_inputs[:1])
    prev_outputs = jnp.concatenate([zero_layer, layer_outputs[:-1]], axis=0)
    prev_multipliers = jnp.concatenate([zero_layer, multipliers[:-1]], axis=0)
    gradient = fit_weight * pulled + prev_multipliers + penalty * (layer_inputs - prev_outputs)
    stepped = layer_inputs - step_input * gradient
    layer_ids = jnp.arange(layer_inputs.shape[0])[:, None, None]
    new_inputs = jnp.where(layer_ids == 0, layer_inputs, stepped)
    weight_grad = fit_weight * scaling * jnp.einsum('lsk,lsd->lkd', misfit, layer_inputs, precision=highest)
    new_weights = weights - step_weight * weight_grad
    new_offsets = offsets - step_offset * fit_weight * lax.optimization_barrier(jnp.sum(misfit, axis=1))
    next_inputs = jnp.concatenate([new_inputs[1:], zero_layer], axis=0)
    is_last = layer_ids == layer_inputs.shape[0] - 1
    coupled = jnp.maximum(0.0, (fit_weight * affine + penalty * next_inputs + multipliers) / (fit_weight + penalty))
    new_outputs = jnp.where(is_last, jnp.maximum(0.0, affine), coupled)
    new_multipliers = jnp.where(is_last, multipliers, multipliers + penalty * (next_inputs - new_outputs))
    return (new_inputs, new_weights, new_offsets, new_outputs, new_multipliers)
```

```python
import math

import jax
import jax.numpy as jnp
from jax import lax
from jax.sharding import PartitionSpec as P

fit_weight = 1.0
penalty = 1.0
step_input = 0.5
PRECISION = lax.Precision.HIGH


def passed_along(block, axis, distance):
    devices = range(lax.axis_size(axis))
    route = [(i - distance, i) for i in devices if i - distance in devices]
    return lax.ppermute(block, axis, route)


def swapped(block, bit):
    route = [(i, i ^ bit) for i in range(lax.axis_size("dp"))]
    return lax.ppermute(block, "dp", route)


def dot(a, b, dims):
    return lax.dot_general(a, b, (dims, ((), ())), precision=PRECISION)


def times_transposed(a, b):
    return dot(a, b, ((1,), (1,)))


def times(a, b):
    return dot(a, b, ((1,), (0,)))


def transposed_times(a, b):
    return dot(a, b, ((0,), (0,)))


def finish(inputs, outputs, mults, drive, prev_drive, affine, pulled_step, next_step):
    layer_index = lax.axis_index("depth")
    is_first = layer_index == 0
    is_last = layer_index == lax.axis_size("depth") - 1
    inputs_new = jnp.where(is_first, inputs, pulled_step - step_input * prev_drive)
    next_inputs = next_step - step_input * drive
    coupled = jnp.maximum(
        0.0, (fit_weight * affine + penalty * next_inputs + mults) / (fit_weight + penalty)
    )
    outputs_new = jnp.where(is_last, jnp.maximum(0.0, affine), coupled)
    mults_new = jnp.where(is_last, mults, mults + penalty * (next_inputs - outputs_new))
    return inputs_new, outputs_new, mults_new


def body_general(layer_inputs, weights, offsets, layer_outputs, multipliers):
    inputs, outputs, mults = layer_inputs[0], layer_outputs[0], multipliers[0]
    scaling = 1.0 / math.sqrt(inputs.shape[1])
    samples = inputs.shape[0] * lax.axis_size("dp")
    step_weight = 8.0 / math.sqrt(samples)
    step_offset = 0.5 / math.sqrt(samples)
    drive = mults - penalty * outputs
    prev_drive = passed_along(drive, "depth", 1)
    weight = lax.all_gather(weights[0], "dp", axis=0, tiled=True)
    offset = lax.all_gather(offsets, "dp", axis=1, tiled=True)
    affine = scaling * times_transposed(inputs, weight) + offset
    misfit = affine - outputs
    weight_grad = fit_weight * scaling * transposed_times(misfit, inputs)
    weight_sum = lax.psum_scatter(weight_grad, "dp", scatter_dimension=0, tiled=True)
    offset_sum = lax.psum_scatter(
        fit_weight * jnp.sum(misfit, axis=0), "dp", scatter_dimension=0, tiled=True
    )
    pulled = scaling * times(misfit, weight)
    pulled_step = inputs - step_input * (fit_weight * pulled + penalty * inputs)
    next_step = passed_along(pulled_step, "depth", -1)
    inputs_new, outputs_new, mults_new = finish(
        inputs, outputs, mults, drive, prev_drive, affine, pulled_step, next_step
    )
    weights_new = weights - step_weight * weight_sum[None]
    offsets_new = offsets - step_offset * offset_sum[None]
    return inputs_new[None], weights_new, offsets_new, outputs_new[None], mults_new[None]


def body_square(layer_inputs, weights, offsets, layer_outputs, multipliers):
    inputs, outputs, mults = layer_inputs[0], layer_outputs[0], multipliers[0]
    rows, width = inputs.shape
    units = weights.shape[1]
    half = units // 2
    scaling = 1.0 / math.sqrt(width)
    samples = rows * lax.axis_size("dp")
    step_weight = 8.0 / math.sqrt(samples)
    step_offset = 0.5 / math.sqrt(samples)
    me = lax.axis_index("dp")

    w_own = weights[0]
    low_own, high_own = w_own[:half], w_own[half:]
    low_own, high_own, inputs = lax.optimization_barrier((low_own, high_own, inputs))
    low_x, high_y = swapped(low_own, 2), swapped(high_own, 4)
    inputs_other = swapped(inputs, 1)
    inputs_other, outputs_late = lax.optimization_barrier((inputs_other, outputs))
    drive = mults - penalty * outputs
    prev_drive = passed_along(drive, "depth", 1)
    b_own = offsets
    b_x, b_y, b_d = swapped(b_own, 2), swapped(b_own, 4), swapped(b_own, 6)

    def columns(array, index):
        return lax.dynamic_slice(array, (0, index * units), (rows, units))

    def arranged(own, x, y, d):
        joined_a = jnp.concatenate([x[:, :half], y[:, half:]], axis=1)
        joined_b = jnp.concatenate([x[:, half:], y[:, :half]], axis=1)
        return own, joined_a, d, joined_b

    flips = (0, 2, 4, 6)
    out_mine = arranged(*[columns(outputs_late, me ^ f) for f in flips])
    out_sent = arranged(*[columns(outputs_late, me ^ f ^ 1) for f in flips])
    out_other = swapped(jnp.concatenate(out_sent, axis=1), 1)
    biases = arranged(b_own, b_x, b_y, b_d)
    both = jnp.concatenate([inputs, inputs_other], axis=0)

    def layer(n, w):
        affine = scaling * times_transposed(both, w) + biases[n]
        target = jnp.concatenate([out_mine[n], out_other[:, n * units : (n + 1) * units]], axis=0)
        return affine, affine - target

    affine_own, m = layer(0, w_own)
    g_own = transposed_times(m, both)
    o_own = jnp.sum(m, axis=0, keepdims=True)
    pulled = times(m, w_own)
    low_x, high_y, g_own, pulled, o_own = lax.optimization_barrier(
        (low_x, high_y, g_own, pulled, o_own)
    )

    low_d, high_d = swapped(low_x, 4), swapped(high_y, 2)
    w_a = jnp.concatenate([low_x, high_y], axis=0)
    affine_a, m = layer(1, w_a)
    g_a = transposed_times(m, both)
    o_a = jnp.sum(m, axis=0, keepdims=True)
    pulled = pulled + times(m, w_a)
    low_d, high_d, g_a, pulled, o_a, low_own, high_own = lax.optimization_barrier(
        (low_d, high_d, g_a, pulled, o_a, low_own, high_own)
    )

    high_x, low_y = swapped(high_own, 2), swapped(low_own, 4)
    w_d = jnp.concatenate([low_d, high_d], axis=0)
    affine_d, m = layer(2, w_d)
    g_d = transposed_times(m, both)
    o_d = jnp.sum(m, axis=0, keepdims=True)
    pulled = pulled + times(m, w_d)
    high_x, low_y, g_a, g_d, pulled, o_d, prev_drive = lax.optimization_barrier(
        (high_x, low_y, g_a, g_d, pulled, o_d, prev_drive)
    )

    x_low, y_high = swapped(g_a[:half], 2), swapped(g_a[half:], 4)
    from_x, from_y = swapped(g_d[:half], 2), swapped(g_d[half:], 4)
    w_b = jnp.concatenate([high_x, low_y], axis=0)
    affine_b, m = layer(3, w_b)
    pulled_other = swapped(pulled[rows:] + times(m[rows:], w_b), 1)
    pulled_mine = pulled[:rows] + times(m[:rows], w_b)
    pulled_all = scaling * (pulled_mine + pulled_other)
    pulled_step = inputs - step_input * (fit_weight * pulled_all + penalty * inputs)
    m, pulled_step = lax.optimization_barrier((m, pulled_step))
    next_step = passed_along(pulled_step, "depth", -1)
    g_b = transposed_times(m, both)
    o_b = jnp.sum(m, axis=0, keepdims=True)

    x_high = swapped(g_b[:half] + from_y, 2)
    y_low = swapped(g_b[half:] + from_x, 4)
    sum_low = g_own[:half] + x_low + y_low
    sum_high = g_own[half:] + x_high + y_high
    weight_step = step_weight * fit_weight * scaling
    weights_new = w_own - weight_step * jnp.concatenate([sum_low, sum_high], axis=0)
    o_x = jnp.concatenate([o_a[:, :half], o_b[:, :half]], axis=1)
    o_y = jnp.concatenate([o_b[:, half:], o_a[:, half:]], axis=1)
    offset_sum = o_own + swapped(o_x, 2) + swapped(o_y, 4) + swapped(o_d, 6)
    offsets_new = offsets - step_offset * fit_weight * offset_sum

    affines = (affine_own, affine_a, affine_d, affine_b)
    affine_other = swapped(jnp.concatenate([a[rows:] for a in affines], axis=1), 1)

    def by_owner(own, a, d, b):
        x = jnp.concatenate([a[:, :half], b[:, :half]], axis=1)
        y = jnp.concatenate([b[:, half:], a[:, half:]], axis=1)
        return own, x, y, d

    mine = by_owner(*[a[:rows] for a in affines])
    other = by_owner(*[affine_other[:, n * units : (n + 1) * units] for n in range(len(flips))])
    affine = jnp.zeros_like(outputs)
    for n, f in enumerate(flips):
        affine = lax.dynamic_update_slice(affine, mine[n], (0, (me ^ f) * units))
        affine = lax.dynamic_update_slice(affine, other[n], (0, (me ^ f ^ 1) * units))
    inputs_new, outputs_new, mults_new = finish(
        inputs, outputs, mults, drive, prev_drive, affine, pulled_step, next_step
    )
    return (
        inputs_new[None],
        weights_new[None],
        offsets_new,
        outputs_new[None],
        mults_new[None],
    )


def solution(mesh):
    specs = (
        P("depth", "dp", None),
        P("depth", "dp", None),
        P("depth", "dp"),
        P("depth", "dp", None),
        P("depth", "dp", None),
    )
    body = body_square if mesh.shape["dp"] == 8 else body_general
    return jax.shard_map(body, mesh=mesh, in_specs=specs, out_specs=specs, check_vma=False)
```

```python
import math

import jax
import jax.numpy as jnp
from jax import lax
from jax.sharding import PartitionSpec as P


fit_weight = 1.0
penalty = 1.0
step_input = 0.5
PRECISION = lax.Precision.HIGH


def passed_along(block, axis, distance):
    devices = range(lax.axis_size(axis))
    route = [(i - distance, i) for i in devices if i - distance in devices]
    return lax.ppermute(block, axis, route)


def swapped(block, bit):
    route = [(i, i ^ bit) for i in range(lax.axis_size("dp"))]
    return lax.ppermute(block, "dp", route)


def dot(a, b, dims):
    return lax.dot_general(a, b, (dims, ((), ())), precision=PRECISION)


def times_transposed(a, b):
    return dot(a, b, ((1,), (1,)))


def times(a, b):
    return dot(a, b, ((1,), (0,)))


def transposed_times(a, b):
    return dot(a, b, ((0,), (0,)))


def finish(inputs, mults, drive, prev_drive, affine, pulled_step, next_step):
    layer_index = lax.axis_index("depth")
    is_first = layer_index == 0
    is_last = layer_index == lax.axis_size("depth") - 1
    inputs_new = jnp.where(is_first, inputs, pulled_step - step_input * prev_drive)
    next_inputs = next_step - step_input * drive
    coupled = jnp.maximum(
        0.0, (fit_weight * affine + penalty * next_inputs + mults) / (fit_weight + penalty)
    )
    outputs_new = jnp.where(is_last, jnp.maximum(0.0, affine), coupled)
    mults_new = jnp.where(is_last, mults, mults + penalty * (next_inputs - outputs_new))
    return inputs_new, outputs_new, mults_new


def body_general(layer_inputs, weights, offsets, layer_outputs, multipliers):
    inputs, outputs, mults = layer_inputs[0], layer_outputs[0], multipliers[0]
    scaling = 1.0 / math.sqrt(inputs.shape[1])
    samples = inputs.shape[0] * lax.axis_size("dp")
    step_weight = 8.0 / math.sqrt(samples)
    step_offset = 0.5 / math.sqrt(samples)
    drive = mults - penalty * outputs
    prev_drive = passed_along(drive, "depth", 1)
    weight = lax.all_gather(weights[0], "dp", axis=0, tiled=True)
    offset = lax.all_gather(offsets, "dp", axis=1, tiled=True)
    affine = scaling * times_transposed(inputs, weight) + offset
    misfit = affine - outputs
    weight_grad = fit_weight * scaling * transposed_times(misfit, inputs)
    weight_sum = lax.psum_scatter(weight_grad, "dp", scatter_dimension=0, tiled=True)
    offset_sum = lax.psum_scatter(
        fit_weight * jnp.sum(misfit, axis=0), "dp", scatter_dimension=0, tiled=True
    )
    pulled = scaling * times(misfit, weight)
    pulled_step = inputs - step_input * (fit_weight * pulled + penalty * inputs)
    next_step = passed_along(pulled_step, "depth", -1)
    inputs_new, outputs_new, mults_new = finish(
        inputs, mults, drive, prev_drive, affine, pulled_step, next_step
    )
    weights_new = weights - step_weight * weight_sum[None]
    offsets_new = offsets - step_offset * offset_sum[None]
    return inputs_new[None], weights_new, offsets_new, outputs_new[None], mults_new[None]


def body_square(layer_inputs, weights, offsets, layer_outputs, multipliers):
    inputs, outputs, mults = layer_inputs[0], layer_outputs[0], multipliers[0]
    rows, width = inputs.shape
    units = weights.shape[1]
    half = units // 2
    scaling = 1.0 / math.sqrt(width)
    samples = rows * lax.axis_size("dp")
    step_weight = 8.0 / math.sqrt(samples)
    step_offset = 0.5 / math.sqrt(samples)
    me = lax.axis_index("dp")

    w_own = weights[0]
    low_own, high_own = w_own[:half], w_own[half:]
    low_own, high_own, inputs = lax.optimization_barrier((low_own, high_own, inputs))
    low_x, high_y = swapped(low_own, 2), swapped(high_own, 4)
    inputs_other = swapped(inputs, 1)
    inputs_other, outputs_late, b_own = lax.optimization_barrier((inputs_other, outputs, offsets))
    drive = mults - penalty * outputs
    prev_drive = passed_along(drive, "depth", 1)
    b_x, b_y, b_d = swapped(b_own, 2), swapped(b_own, 4), swapped(b_own, 6)

    def columns(array, index):
        return lax.dynamic_slice(array, (0, index * units), (rows, units))

    def arranged(own, x, y, d):
        joined_a = jnp.concatenate([x[:, :half], y[:, half:]], axis=1)
        joined_b = jnp.concatenate([x[:, half:], y[:, :half]], axis=1)
        return own, joined_a, d, joined_b

    flips = (0, 2, 4, 6)
    out_mine = arranged(*[columns(outputs_late, me ^ f) for f in flips])
    out_sent = arranged(*[columns(outputs_late, me ^ f ^ 1) for f in flips])
    out_other = swapped(jnp.concatenate(out_sent, axis=1), 1)
    biases = arranged(b_own, b_x, b_y, b_d)
    both = jnp.concatenate([inputs, inputs_other], axis=0)

    def layer(n, w):
        affine = scaling * times_transposed(both, w) + biases[n]
        target = jnp.concatenate([out_mine[n], out_other[:, n * units : (n + 1) * units]], axis=0)
        return affine, affine - target

    low_x, high_y, both, out_other = lax.optimization_barrier((low_x, high_y, both, out_other))

    low_d, high_d = swapped(low_x, 4), swapped(high_y, 2)
    w_a = jnp.concatenate([low_x, high_y], axis=0)
    affine_own, m_own = layer(0, w_own)
    affine_a, m = layer(1, w_a)
    g_a = transposed_times(m, both)
    o_a = jnp.sum(m, axis=0, keepdims=True)
    pulled = times(m_own, w_own) + times(m, w_a)
    low_d, high_d, g_a, pulled, m_own, low_own, high_own = lax.optimization_barrier(
        (low_d, high_d, g_a, pulled, m_own, low_own, high_own)
    )

    high_x, low_y = swapped(high_own, 2), swapped(low_own, 4)
    w_d = jnp.concatenate([low_d, high_d], axis=0)
    affine_d, m = layer(2, w_d)
    g_d = transposed_times(m, both)
    o_d = jnp.sum(m, axis=0, keepdims=True)
    pulled = pulled + times(m, w_d)
    g_own = transposed_times(m_own, both)
    o_own = jnp.sum(m_own, axis=0, keepdims=True)
    high_x, low_y, g_a, g_d, g_own, pulled, prev_drive = lax.optimization_barrier(
        (high_x, low_y, g_a, g_d, g_own, pulled, prev_drive)
    )

    x_low, y_high = swapped(g_a[:half], 2), swapped(g_a[half:], 4)
    from_x, from_y = swapped(g_d[:half], 2), swapped(g_d[half:], 4)
    w_b = jnp.concatenate([high_x, low_y], axis=0)
    affine_b, m = layer(3, w_b)
    pulled_other = swapped(pulled[rows:] + times(m[rows:], w_b), 1)
    pulled_mine = pulled[:rows] + times(m[:rows], w_b)
    pulled_all = scaling * (pulled_mine + pulled_other)
    pulled_step = inputs - step_input * (fit_weight * pulled_all + penalty * inputs)
    m, pulled_step, affine_own, affine_a, affine_d, affine_b = lax.optimization_barrier(
        (m, pulled_step, affine_own, affine_a, affine_d, affine_b)
    )
    next_step = passed_along(pulled_step, "depth", -1)
    g_b = transposed_times(m, both)
    o_b = jnp.sum(m, axis=0, keepdims=True)

    x_high = swapped(g_b[:half] + from_y, 2)
    y_low = swapped(g_b[half:] + from_x, 4)
    sum_low = g_own[:half] + x_low + y_low
    sum_high = g_own[half:] + x_high + y_high
    weight_step = step_weight * fit_weight * scaling
    weights_new = w_own - weight_step * jnp.concatenate([sum_low, sum_high], axis=0)
    o_x = jnp.concatenate([o_a[:, :half], o_b[:, :half]], axis=1)
    o_y = jnp.concatenate([o_b[:, half:], o_a[:, half:]], axis=1)
    offset_sum = o_own + swapped(o_x, 2) + swapped(o_y, 4) + swapped(o_d, 6)
    offsets_new = offsets - step_offset * fit_weight * offset_sum

    affines = (affine_own, affine_a, affine_d, affine_b)
    affine_other = swapped(jnp.concatenate([a[rows:] for a in affines], axis=1), 1)

    def by_owner(own, a, d, b):
        x = jnp.concatenate([a[:, :half], b[:, :half]], axis=1)
        y = jnp.concatenate([b[:, half:], a[:, half:]], axis=1)
        return own, x, y, d

    mine = by_owner(*[a[:rows] for a in affines])
    other = by_owner(*[affine_other[:, n * units : (n + 1) * units] for n in range(len(flips))])
    affine = jnp.zeros_like(outputs)
    for n, f in enumerate(flips):
        affine = lax.dynamic_update_slice(affine, mine[n], (0, (me ^ f) * units))
        affine = lax.dynamic_update_slice(affine, other[n], (0, (me ^ f ^ 1) * units))
    inputs_new, outputs_new, mults_new = finish(
        inputs, mults, drive, prev_drive, affine, pulled_step, next_step
    )
    return (
        inputs_new[None],
        weights_new[None],
        offsets_new,
        outputs_new[None],
        mults_new[None],
    )


def solution(mesh):
    specs = (
        P("depth", "dp", None),
        P("depth", "dp", None),
        P("depth", "dp"),
        P("depth", "dp", None),
        P("depth", "dp", None),
    )
    square = mesh.shape["dp"] == 8
    body = body_square if square else body_general
    return jax.shard_map(body, mesh=mesh, in_specs=specs, out_specs=specs, check_vma=False)
```
